32 devices in a mesh: expert: 4 (over y, x), shard: 8 (over z, core).
Axes of the slice: x: 2, y: 2, z: 4, core: 2. Of those that a mesh axis runs over, the one named last changes fastest.
Arguments:
- hidden: bfloat16 [64, 4096], P('shard'), may hold values from -6 to 6
- queries: bfloat16 [64, 32, 128], P('shard', 'expert'), may hold values from -30 to 30
- key_cache: bfloat16 [64, 512, 8, 128], P('shard', None, 'expert'), may hold values from -16 to 16
- value_cache: bfloat16 [64, 512, 8, 128], P('shard', None, 'expert'), may hold values from -6 to 6
- out_weight: bfloat16 [4096, 4096], P('expert', 'shard'), may hold values from -0.09375 to 0.09375
- norm_gain: bfloat16 [4096], replicated, may hold values from 0.099609375 to 1.8984375
- router: bfloat16 [4096, 8], replicated, may hold values from -0.09375 to 0.09375
- expert_ids: int32 [64, 2], replicated, may hold values from 0 to 7, all different within a row; in each aligned block of 64 rows (0 to 63, 64 to 127, ...) at most 32 rows name the same one
- gate_weight: bfloat16 [8, 4096, 14336], P('expert', None, 'shard'), may hold values from -0.09375 to 0.09375
- up_weight: bfloat16 [8, 4096, 14336], P('expert', None, 'shard'), may hold values from -0.09375 to 0.09375
- down_weight: bfloat16 [8, 14336, 4096], P('expert', 'shard'), may hold values from -0.046875 to 0.046875
Outputs:
- layer_out: bfloat16 [64, 4096], P('shard')
The draws below stay inside these ranges and needn't reach their ends.
Inputs may be any that keep to these rules, and one draw needn't show every extreme that they name: `expert_ids`: each token names two different experts; over all 64 tokens no expert is named by more than 32 tokens, a bound that some block reaches.
All inputs are finite; a program needn't handle non-finite values.
Results may differ from the reference program's by a relative error of at most 0.008.
Values may be sent and summed in bfloat16 or wider, within the bound.
A program may use at most 128 MiB of HBM per device.

```python
import math
import jax
import jax.numpy as jnp
import numpy as np
from jax import lax

D = 4096
FF = 14336
EXPERTS = 8
HEADS = 32
KV_HEADS = 8
HD = 128
POS = 512
TOKENS = 64
CAP = 32


def shared_attention(key):
    base_key = jax.random.fold_in(key, 7)
    key_query, key_rows = jax.random.split(base_key, 2)
    query_draw = jnp.clip(jax.random.normal(key_query, (TOKENS, HEADS, HD), jnp.float32), -4.0, 4.0)
    key_draw = jnp.clip(jax.random.normal(key_rows, (TOKENS, POS, KV_HEADS, HD), jnp.float32), -4.0, 4.0)
    return (query_draw, key_draw)


def draw_queries(key, part):
    return shared_attention(key)[0].astype(jnp.bfloat16)


def draw_key_cache(key, part):
    return shared_attention(key)[1].astype(jnp.bfloat16)


def levels(key, dims, cuts, smallest, high):
    def one(axis_at, shards_of):
        heights = jax.random.uniform(jax.random.fold_in(jax.random.fold_in(key, 6), axis_at), (shards_of,), jnp.float32, smallest / len(cuts), high / len(cuts))
        return jnp.repeat(jnp.exp(heights), dims[axis_at] // shards_of).reshape((-1,) + (1,) * (len(dims) - axis_at - 1))

    factor_of = one(*cuts[0])
    for cut in cuts[1:]:
        factor_of = factor_of * one(*cut)
    return factor_of


def routed_block(stream_key, own, number, rows, amount, top, most, skew):
    sequence = jax.random.permutation(stream_key, amount)
    packed, common = shares(amount, rows * top, most, skew, True), shares(amount, rows * top, most, skew, False)
    places = jnp.arange(amount)

    def named(tallies, rotation):
        used = int((tallies > 0).sum())
        fixed = max(1, used // 4)
        shifted = fixed + (places - fixed + rotation * (used - fixed)) % max(1, amount - fixed)
        return jnp.zeros((amount,), jnp.int32).at[sequence[jnp.where(places < fixed, places, shifted)]].set(jnp.asarray(tallies, jnp.int32))

    tallies = jnp.where(number % 4 == 0, named(packed, number // 4), named(common, number - number // 4 - 1))
    mixed = jax.random.permutation(jax.random.fold_in(own, 3), amount)
    source_of, sink = mixed[0:amount // 2 * 2:2], mixed[1:amount // 2 * 2:2]
    margin = jnp.minimum(tallies[source_of] - 1, most - tallies[sink]) // 2
    margin = jnp.where((source_of == sequence[0]) | (sink == sequence[0]) | (tallies[sink] == 0), 0, jnp.maximum(margin, 0))
    shifted = jax.random.randint(jax.random.fold_in(own, 4), (amount // 2,), 0, 1 << 20) % (margin + 1)
    tallies = tallies.at[source_of].add(-shifted).at[sink].add(shifted)
    items = jnp.searchsorted(jnp.cumsum(tallies), jnp.arange(rows * top), side="right").astype(jnp.int32)
    table = items.reshape(top, rows).T
    table = table[jax.random.permutation(jax.random.fold_in(own, 1), rows)]
    rotation = jax.random.randint(jax.random.fold_in(own, 2), (rows, 1), 0, top)
    return jnp.take_along_axis(table, (jnp.arange(top)[None, :] + rotation) % top, axis=1)


def shares(count, total, most, lean, full):
    portions = [(1 << 20) // math.isqrt(grade ** lean) + 1 for grade in range(1, count + 1)]
    largest = most if full else min(most, max(-(-total // count), total * portions[0] // sum(portions)))
    least = 1 if total - largest >= count - 1 else 0
    counts, surplus = [largest] + [least] * (count - 1), total - largest - least * (count - 1)
    while surplus > 0:
        candidates = [i for i in range(1, count) if counts[i] < largest] or [i for i in range(1, count) if counts[i] < most]
        mass, budget = sum([portions[i] for i in candidates]), surplus
        for i in candidates:
            extra = min(most - counts[i], max(1, budget * portions[i] // mass), surplus)
            counts[i] = counts[i] + extra
            surplus = surplus - extra
    return np.array(counts)


def gaussian(stream_key, dims, spread, limit, cuts=(), held_as=jnp.bfloat16):
    values = spread * jax.random.normal(stream_key, dims, jnp.float32)
    if cuts:
        values = values * levels(stream_key, dims, cuts, -0.22, 0.18)
    return jnp.clip(values, -limit, limit).astype(held_as)


def setup_inputs(seed: int = 0) -> dict:
    key_list = jax.random.split(jax.random.key(seed), 12)
    hidden = gaussian(key_list[0], (TOKENS, D), 1.0, 6.0, ((0, 8),))
    queries = draw_queries(jax.random.fold_in(key_list[11], 71), 0)
    key_cache = draw_key_cache(jax.random.fold_in(key_list[11], 71), 0)
    value_cache = gaussian(key_list[3], (TOKENS, POS, KV_HEADS, HD), 1.0, 6.0, ((0, 8), (2, 4)))
    out_weight = gaussian(key_list[4], (HEADS * HD, D), (HEADS * HD) ** -0.5, 0.09375, ((0, 4), (1, 8)))
    norm_gain = jnp.clip(1.0 + 0.18 * jax.random.normal(key_list[5], (D,), jnp.float32), 0.099609375, 1.8984375).astype(jnp.bfloat16)
    router = gaussian(key_list[6], (D, EXPERTS), D ** -0.5, 0.09375)
    expert_ids_keys = jax.random.split(jax.random.fold_in(key_list[7], 1), TOKENS // TOKENS)
    expert_ids_turns = jax.random.permutation(jax.random.fold_in(key_list[7], 3), TOKENS // TOKENS)
    expert_ids = jax.vmap(lambda own, number: routed_block(jax.random.fold_in(key_list[7], 2), own, number, TOKENS, EXPERTS, 2, CAP, 2))(expert_ids_keys, expert_ids_turns).reshape((TOKENS, 2))
    gate_weight = gaussian(key_list[8], (EXPERTS, D, FF), D ** -0.5, 0.09375, ((0, 4), (2, 8)))
    up_weight = gaussian(key_list[9], (EXPERTS, D, FF), D ** -0.5, 0.09375, ((0, 4), (2, 8)))
    down_weight = gaussian(key_list[10], (EXPERTS, FF, D), FF ** -0.5, 0.046875, ((0, 4), (1, 8)))
    return {"hidden": hidden, "queries": queries, "key_cache": key_cache, "value_cache": value_cache, "out_weight": out_weight, "norm_gain": norm_gain, "router": router, "expert_ids": expert_ids, "gate_weight": gate_weight, "up_weight": up_weight, "down_weight": down_weight}


def reference(hidden, queries, key_cache, value_cache, out_weight, norm_gain, router, expert_ids, gate_weight, up_weight, down_weight):
    per_kv = HEADS // KV_HEADS
    query_blocks = queries.astype(jnp.float32).reshape(TOKENS, KV_HEADS, per_kv, HD)
    scores = jnp.einsum('tkgd,tpkd->tkgp', query_blocks, key_cache.astype(jnp.float32)) / math.sqrt(HD)
    attn_weights = jax.nn.softmax(scores, axis=-1).astype(jnp.bfloat16)
    attended = jnp.einsum('tkgp,tpkd->tkgd', attn_weights.astype(jnp.float32), value_cache.astype(jnp.float32))
    attended = attended.astype(jnp.bfloat16).reshape(TOKENS, HEADS * HD)
    stream = hidden.astype(jnp.float32) + jnp.dot(attended, out_weight, preferred_element_type=jnp.float32)
    scaled = stream * lax.rsqrt(lax.optimization_barrier(jnp.mean(stream * stream, axis=-1, keepdims=True)) + 1e-05)
    normed = (scaled * norm_gain.astype(jnp.float32)).astype(jnp.bfloat16)
    logits = jnp.dot(normed, router, preferred_element_type=jnp.float32)
    top_first = jnp.take_along_axis(logits, expert_ids[:, 0:1], axis=1)[:, 0]
    top_second = jnp.take_along_axis(logits, expert_ids[:, 1:2], axis=1)[:, 0]
    weight_first = 1.0 / (1.0 + jnp.exp(top_second - top_first))
    weight_second = 1.0 / (1.0 + jnp.exp(top_first - top_second))

    def expert_step(summed, expert):
        gated = jnp.dot(normed, gate_weight[expert], preferred_element_type=jnp.float32)
        upward = jnp.dot(normed, up_weight[expert], preferred_element_type=jnp.float32)
        activated = (jax.nn.silu(gated) * upward).astype(jnp.bfloat16)
        expert_out = jnp.dot(activated, down_weight[expert], preferred_element_type=jnp.float32)
        routed_weight = jnp.where(expert_ids[:, 0] == expert, weight_first, 0.0) + jnp.where(expert_ids[:, 1] == expert, weight_second, 0.0)
        return (summed + routed_weight[:, None] * expert_out, None)
    start_sum = jnp.zeros((TOKENS, D), jnp.float32)
    expert_mix, _ = lax.scan(expert_step, start_sum, jnp.arange(EXPERTS, dtype=jnp.int32))
    return (stream + expert_mix).astype(jnp.bfloat16)
```

```python
import functools
import math

import jax
import jax.numpy as jnp
from jax import lax
from jax.experimental import pallas as pl
from jax.experimental.pallas import tpu as pltpu
from jax.sharding import PartitionSpec as P

F32 = jnp.float32
BF16 = jnp.bfloat16
VMEM_BYTES = 61 * 1024 * 1024
DOWN = 256
LAG = 2


def layer_kernel(
    sizes,
    hidden_ref,
    queries_ref,
    key_ref,
    value_ref,
    out_weight_ref,
    gain_ref,
    router_ref,
    ids_ref,
    gate_ref,
    up_ref,
    down_ref,
    out_ref,
    ring,
    keys,
    values,
    proj,
    score,
    heads,
    att_all,
    hid_all,
    part_all,
    stream,
    owned,
    x_all,
    normed,
    route,
    act,
    part_out,
    part_in,
    group,
    ring_sem,
    kv_sem,
    proj_sem,
    att_s,
    att_r,
    hid_s,
    hid_r,
    part_s,
    part_r,
    x_s,
    x_r,
    own_s,
    own_r,
    a_s,
    a_r,
    b_s,
    b_r,
):
    shards, groups, depth, width, kv_local = sizes
    me = lax.axis_index("shard")
    ge = lax.axis_index("expert")
    count, features = hidden_ref.shape
    tokens = count * shards
    cols = features // shards
    members, _, hidden_units = gate_ref.shape
    per_member = hidden_units // width
    gu_pairs = members * per_member
    chunk = 2 * DOWN
    chunks = features // chunk
    total = gu_pairs + chunks
    heads_local, head_size = queries_ref.shape[1:]
    per_kv = heads_local // kv_local

    def shard_peer(d):
        return lax.rem(me + d, shards)

    def group_peer(d):
        return lax.rem(ge + d, groups)

    def to_shard(src, dst, ssem, rsem, peer):
        return pltpu.make_async_remote_copy(
            src_ref=src, dst_ref=dst, send_sem=ssem, recv_sem=rsem,
            device_id={"shard": peer}, device_id_type=pl.DeviceIdType.MESH,
        )

    def to_group(src, dst, ssem, rsem, peer):
        return pltpu.make_async_remote_copy(
            src_ref=src, dst_ref=dst, send_sem=ssem, recv_sem=rsem,
            device_id={"expert": peer}, device_id_type=pl.DeviceIdType.MESH,
        )

    def each(n, body):
        def step(i, carry):
            body(i)
            return carry

        lax.fori_loop(0, n, step, 0)

    def span(i, size):
        return pl.ds(pl.multiple_of(i * size, size), size)

    def gate_up_copies(pair):
        slot = lax.rem(pair, depth)
        member, j = lax.div(pair, per_member), lax.rem(pair, per_member)
        where = slice(None) if per_member == 1 else span(j, width)
        return [
            pltpu.make_async_copy(
                ref.at[member, :, where], ring.at[slot, k, 0:features, 0:width], ring_sem.at[slot, k]
            )
            for k, ref in enumerate((gate_ref, up_ref))
        ]

    def down_copies(pair):
        slot = lax.rem(pair, depth)
        c = pair - gu_pairs
        return [
            pltpu.make_async_copy(
                down_ref.at[m, :, span(2 * c + k, DOWN)],
                ring.at[slot, k, m * hidden_units:(m + 1) * hidden_units, 0:DOWN],
                ring_sem.at[slot, k * members + m],
            )
            for k in range(2)
            for m in range(members)
        ]

    def start_pair(pair):
        @pl.when(pair < gu_pairs)
        def _():
            for copy in gate_up_copies(pair):
                copy.start()

        @pl.when(jnp.logical_and(pair >= gu_pairs, pair < total))
        def _():
            for copy in down_copies(pair):
                copy.start()

    barrier = pltpu.get_barrier_semaphore()
    each(shards - 1, lambda d: pl.semaphore_signal(
        barrier, 1, device_id={"shard": shard_peer(d + 1)}, device_id_type=pl.DeviceIdType.MESH))
    each(groups - 1, lambda d: pl.semaphore_signal(
        barrier, 1, device_id={"expert": group_peer(d + 1)}, device_id_type=pl.DeviceIdType.MESH))

    def key_copy(t):
        return pltpu.make_async_copy(key_ref.at[t], keys.at[t], kv_sem.at[0, t])

    def value_copy(t):
        return pltpu.make_async_copy(value_ref.at[t], values.at[t], kv_sem.at[1, t])

    each(count, lambda t: key_copy(t).start())
    each(count, lambda t: value_copy(t).start())
    proj_copy = pltpu.make_async_copy(out_weight_ref, proj, proj_sem)
    proj_copy.start()
    each(depth, start_pair)

    for t in range(count):
        key_copy(t).wait()
        score[t * heads_local:(t + 1) * heads_local, :] = lax.dot_general(
            queries_ref[t], keys[t], (((1,), (1,)), ((), ())), preferred_element_type=F32
        )
    s = score[...] * (1.0 / math.sqrt(head_size))
    row = lax.broadcasted_iota(jnp.int32, s.shape, 0)
    col = lax.broadcasted_iota(jnp.int32, s.shape, 1)
    mine = lax.rem(col, kv_local) == lax.div(lax.rem(row, heads_local), per_kv)
    s = jnp.where(mine, s, -1e30)
    e = jnp.exp(s - jnp.max(s, axis=1, keepdims=True))
    score[...] = e / jnp.sum(e, axis=1, keepdims=True)
    for t in range(count):
        value_copy(t).wait()
        attended = jnp.dot(
            score[t * heads_local:(t + 1) * heads_local, :].astype(BF16), values[t],
            preferred_element_type=F32,
        )
        for h in range(heads_local):
            heads[t:t + 1, h * head_size:(h + 1) * head_size] = attended[h:h + 1, :]
    att_all[me] = heads[...].astype(BF16)

    pl.semaphore_wait(barrier, shards - 1 + groups - 1)

    def att_copy(slot, peer, k):
        return to_shard(att_all.at[slot], att_all.at[slot], att_s.at[k], att_r.at[slot], peer)

    def hid_copy(peer, slot, k):
        return to_shard(
            hidden_ref.at[:, span(peer, cols)], hid_all.at[slot], hid_s.at[k], hid_r.at[slot], peer
        )

    def send_first(d):
        att_copy(me, shard_peer(d + 1), d).start()

    def send_hidden(d):
        hid_copy(shard_peer(d + 1), me, d).start()

    each(shards - 1, send_first)
    each(shards - 1, send_hidden)
    hid_all[me] = hidden_ref[:, span(me, cols)]
    proj_copy.wait()
    each(shards - 1, lambda d: att_copy(shard_peer(d + 1), me, d).wait_recv())

    gathered = att_all[...].astype(F32).reshape(tokens, heads_local * head_size).astype(BF16)
    part_all[ge] = jnp.dot(gathered, proj[...], preferred_element_type=F32).astype(BF16)

    def part_copy(slot, peer, k):
        return to_group(part_all.at[slot], part_all.at[slot], part_s.at[k], part_r.at[slot], peer)

    each(groups - 1, lambda d: part_copy(ge, group_peer(d + 1), d).start())
    each(shards - 1, lambda d: hid_copy(me, shard_peer(d + 1), d).wait_recv())
    each(groups - 1, lambda d: part_copy(group_peer(d + 1), ge, d).wait_recv())
    summed = hid_all[...].astype(F32).reshape(tokens, cols)
    for g in range(groups):
        summed = summed + part_all[g].astype(F32)
    stream[...] = summed
    x_all[:, span(me, cols)] = summed.astype(BF16)

    def x_copy(block, peer, k):
        return to_shard(
            x_all.at[:, span(block, cols)], x_all.at[:, span(block, cols)],
            x_s.at[k], x_r.at[block], peer,
        )

    def own_copy(peer, block, k):
        return to_shard(
            stream.at[span(peer, count), :], owned.at[:, span(block, cols)],
            own_s.at[k], own_r.at[block], peer,
        )

    each(shards - 1, lambda d: x_copy(me, shard_peer(d + 1), d).start())
    each(shards - 1, lambda d: own_copy(shard_peer(d + 1), me, d).start())
    owned[:, span(me, cols)] = stream[span(me, count), :]
    each(shards - 1, lambda d: x_copy(shard_peer(d + 1), me, d).wait_recv())

    square = jnp.zeros((tokens, 1), F32)
    for c in range(chunks):
        x = x_all[:, c * chunk:(c + 1) * chunk].astype(F32)
        square = square + jnp.sum(x * x, axis=1, keepdims=True)
    scale = lax.rsqrt(square / features + 1e-05)
    gain = gain_ref[...].astype(F32)
    lanes = gain.shape[1]
    for c in range(gain.shape[0]):
        part = slice(c * lanes, (c + 1) * lanes)
        normed[:, part] = (x_all[:, part].astype(F32) * scale * gain[c:c + 1]).astype(BF16)

    logits = lax.dot_general(
        normed[...], router_ref[...], (((1,), (1,)), ((), ())), preferred_element_type=F32
    )
    diagonal = lax.broadcasted_iota(jnp.int32, (tokens, tokens), 0) == lax.broadcasted_iota(
        jnp.int32, (tokens, tokens), 1
    )
    first, second = (
        jnp.sum(
            jnp.where(diagonal, ids_ref[k:k + 1, :].astype(F32), 0.0), axis=1, keepdims=True
        ).astype(jnp.int32)
        for k in range(2)
    )
    lane = lax.broadcasted_iota(jnp.int32, logits.shape, 1)
    top_first = jnp.sum(jnp.where(lane == first, logits, 0.0), axis=1, keepdims=True)
    top_second = jnp.sum(jnp.where(lane == second, logits, 0.0), axis=1, keepdims=True)
    weight_first = 1.0 / (1.0 + jnp.exp(top_second - top_first))
    weight_second = 1.0 / (1.0 + jnp.exp(top_first - top_second))
    for m in range(members):
        expert = ge * members + m
        route[m] = jnp.broadcast_to(
            jnp.where(first == expert, weight_first, 0.0)
            + jnp.where(second == expert, weight_second, 0.0),
            (tokens, 128),
        )

    def gate_up(pair):
        slot = lax.rem(pair, depth)
        member, j = lax.div(pair, per_member), lax.rem(pair, per_member)
        for copy in gate_up_copies(pair):
            copy.wait()
        gated = jnp.dot(
            normed[...], ring[slot, 0, 0:features, 0:width], preferred_element_type=F32
        )
        upward = jnp.dot(
            normed[...], ring[slot, 1, 0:features, 0:width], preferred_element_type=F32
        )
        value = gated * (1.0 / (1.0 + jnp.exp(-gated))) * upward * route[member][:, 0:1]
        where = slice(None) if per_member == 1 else span(j, width)
        act[member, :, where] = value.astype(BF16)
        start_pair(pair + depth)

    each(gu_pairs, gate_up)

    def a_copy(c, source, dest, peer, k):
        return to_shard(
            part_out.at[dest, :, span(c, chunk)], part_in.at[source, :, span(c, chunk)],
            a_s.at[k, c], a_r.at[source, c], peer,
        )

    def b_copy(c, slot, peer, k):
        ref = group.at[slot, :, span(c, chunk)]
        return to_group(ref, ref, b_s.at[k, c], b_r.at[slot, c], peer)

    def finish_shards(c):
        each(shards - 1, lambda d: a_copy(c, shard_peer(d + 1), me, me, d).wait_recv())
        mix = part_out[me, :, span(c, chunk)].astype(F32)
        mix = lax.fori_loop(
            1, shards,
            lambda d, got: got + part_in[shard_peer(d), :, span(c, chunk)].astype(F32), mix,
        )
        group[ge, :, span(c, chunk)] = mix.astype(BF16)
        each(groups - 1, lambda d: b_copy(c, ge, group_peer(d + 1), d).start())

    def down(c):
        pair = gu_pairs + c
        slot = lax.rem(pair, depth)
        for copy in down_copies(pair):
            copy.wait()
        for k in range(2):
            y = jnp.zeros((tokens, DOWN), F32)
            for m in range(members):
                y = y + jnp.dot(
                    act[m],
                    ring[slot, k, m * hidden_units:(m + 1) * hidden_units, 0:DOWN],
                    preferred_element_type=F32,
                )
            part_out[:, :, span(2 * c + k, DOWN)] = y.reshape(shards, count, DOWN).astype(BF16)
        each(shards - 1, lambda d: a_copy(c, me, shard_peer(d + 1), shard_peer(d + 1), d).start())
        start_pair(pair + depth)

        @pl.when(c >= LAG)
        def _():
            finish_shards(c - LAG)

    each(chunks, down)
    each(LAG, lambda i: finish_shards(chunks - LAG + i))
    each(shards - 1, lambda d: own_copy(me, shard_peer(d + 1), d).wait_recv())

    def finish(c):
        each(groups - 1, lambda d: b_copy(c, group_peer(d + 1), ge, d).wait_recv())
        result = group[0, :, span(c, chunk)].astype(F32)
        for g in range(1, groups):
            result = result + group[g, :, span(c, chunk)].astype(F32)
        out_ref[:, span(c, chunk)] = (owned[:, span(c, chunk)] + result).astype(BF16)

    each(chunks, finish)

    def sent(d):
        att_copy(me, shard_peer(d + 1), d).wait_send()
        hid_copy(shard_peer(d + 1), me, d).wait_send()
        x_copy(me, shard_peer(d + 1), d).wait_send()
        own_copy(shard_peer(d + 1), me, d).wait_send()
        each(chunks, lambda c: a_copy(c, me, shard_peer(d + 1), shard_peer(d + 1), d).wait_send())

    def sent_group(d):
        part_copy(ge, group_peer(d + 1), d).wait_send()
        each(chunks, lambda c: b_copy(c, ge, group_peer(d + 1), d).wait_send())

    each(shards - 1, sent)
    each(groups - 1, sent_group)


def on_device(
    shards,
    groups,
    hidden,
    queries,
    key_cache,
    value_cache,
    out_weight,
    norm_gain,
    router,
    expert_ids,
    gate_weight,
    up_weight,
    down_weight,
):
    count, features = hidden.shape
    _, heads_local, head_size = queries.shape
    _, positions, kv_local, _ = key_cache.shape
    members, _, hidden_units = gate_weight.shape
    tokens = count * shards
    cols = features // shards
    rows = positions * kv_local
    width = 256 if hidden_units % 256 == 0 else hidden_units
    lanes = max(width, DOWN)
    deep = max(features, members * hidden_units)
    chunks = features // (2 * DOWN)
    total = members * (hidden_units // width) + chunks
    pair_bytes = 2 * 2 * deep * (-(-lanes // 128) * 128)
    fixed = 2 * (
        2 * count * rows * head_size + out_weight.size + 4 * tokens * features
        + (groups + 2) * tokens * cols + members * tokens * hidden_units
        + (2 * count + groups * count) * features + 2 * count * heads_local * rows
    )
    depth = min(total, (VMEM_BYTES - fixed) // pair_bytes)
    sizes = (shards, groups, depth, width, kv_local)
    vmem = pl.BlockSpec(memory_space=pltpu.VMEM)
    hbm = pl.BlockSpec(memory_space=pl.ANY)
    sem = pltpu.SemaphoreType.DMA
    return pl.pallas_call(
        functools.partial(layer_kernel, sizes),
        out_shape=jax.ShapeDtypeStruct((count, features), BF16),
        in_specs=[vmem, vmem, hbm, hbm, hbm, vmem, vmem, vmem, hbm, hbm, hbm],
        out_specs=vmem,
        scratch_shapes=[
            pltpu.VMEM((depth, 2, deep, lanes), BF16),
            pltpu.VMEM((count, rows, head_size), BF16),
            pltpu.VMEM((count, rows, head_size), BF16),
            pltpu.VMEM(out_weight.shape, BF16),
            pltpu.VMEM((count * heads_local, rows), F32),
            pltpu.VMEM((count, heads_local * head_size), F32),
            pltpu.VMEM((shards, count, heads_local * head_size), BF16),
            pltpu.VMEM((shards, count, cols), BF16),
            pltpu.VMEM((groups, tokens, cols), BF16),
            pltpu.VMEM((tokens, cols), F32),
            pltpu.VMEM((count, features), F32),
            pltpu.VMEM((tokens, features), BF16),
            pltpu.VMEM((tokens, features), BF16),
            pltpu.VMEM((members, tokens, 128), F32),
            pltpu.VMEM((members, tokens, hidden_units), BF16),
            pltpu.VMEM((shards, count, features), BF16),
            pltpu.VMEM((shards, count, features), BF16),
            pltpu.VMEM((groups, count, features), BF16),
            sem((depth, 2 * members)),
            sem((2, count)),
            sem,
            sem((shards,)),
            sem((shards,)),
            sem((shards,)),
            sem((shards,)),
            sem((groups,)),
            sem((groups,)),
            sem((shards,)),
            sem((shards,)),
            sem((shards,)),
            sem((shards,)),
            sem((shards, chunks)),
            sem((shards, chunks)),
            sem((groups, chunks)),
            sem((groups, chunks)),
        ],
        compiler_params=pltpu.CompilerParams(
            collective_id=0, has_side_effects=True, vmem_limit_bytes=67043328
        ),
        name="layer",
    )(
        hidden,
        queries,
        key_cache.reshape(count, rows, head_size),
        value_cache.reshape(count, rows, head_size),
        out_weight,
        norm_gain.reshape(features // 128, 128),
        router.T,
        expert_ids.T,
        gate_weight,
        up_weight,
        down_weight,
    )


def solution(mesh):
    in_specs = (
        P("shard", None),
        P("shard", "expert", None),
        P("shard", None, "expert", None),
        P("shard", None, "expert", None),
        P("expert", "shard"),
        P(),
        P(),
        P(),
        P("expert", None, "shard"),
        P("expert", None, "shard"),
        P("expert", "shard", None),
    )
    body = functools.partial(on_device, mesh.shape["shard"], mesh.shape["expert"])
    return jax.shard_map(
        body, mesh=mesh, in_specs=in_specs, out_specs=P("shard", None), check_vma=False
    )
```

```python
import functools
import math

import jax
import jax.numpy as jnp
from jax import lax
from jax.experimental import pallas as pl
from jax.experimental.pallas import tpu as pltpu
from jax.sharding import PartitionSpec as P

F32 = jnp.float32
BF16 = jnp.bfloat16
VMEM_BYTES = 61 * 1024 * 1024
DOWN = 256


def layer_kernel(
    sizes,
    hidden_ref,
    queries_ref,
    key_ref,
    value_ref,
    out_weight_ref,
    gain_ref,
    router_ref,
    ids_ref,
    gate_ref,
    up_ref,
    down_ref,
    out_ref,
    ring,
    keys,
    values,
    proj,
    score,
    heads,
    att_all,
    hid_all,
    part_send,
    part_recv,
    x_all,
    normed,
    route,
    act,
    part_out,
    core_in,
    core_sum,
    chip_in,
    group,
    final,
    ring_sem,
    kv_sem,
    proj_sem,
    att_s,
    att_r,
    hid_s,
    hid_r,
    part_s,
    part_r,
    x_z,
    x_g,
    x_c,
    x_r,
    i_s,
    i_r,
    a_s,
    a_r,
    b_s,
    b_r,
    f_s,
    f_r,
):
    shards, groups, depth, width, kv_local = sizes
    me = lax.axis_index("shard")
    ge = lax.axis_index("expert")
    count, features = hidden_ref.shape
    tokens = count * shards
    cols = features // shards
    members, _, hidden_units = gate_ref.shape
    per_member = hidden_units // width
    gu_pairs = members * per_member
    chunk = 2 * DOWN
    chunks = features // chunk
    total = gu_pairs + chunks
    heads_local, head_size = queries_ref.shape[1:]
    per_kv = heads_local // kv_local
    quarter = shards // groups
    pairs = shards // 2
    core = lax.rem(me, 2)
    chip = lax.div(me, 2)
    sibling = me + 1 - 2 * core

    def shard_peer(d):
        return lax.rem(me + d, shards)

    def group_peer(d):
        return lax.rem(ge + d, groups)

    def chip_peer(d):
        return lax.rem(chip + d, pairs)

    def to_shard(src, dst, ssem, rsem, peer):
        return pltpu.make_async_remote_copy(
            src_ref=src, dst_ref=dst, send_sem=ssem, recv_sem=rsem,
            device_id={"shard": peer}, device_id_type=pl.DeviceIdType.MESH,
        )

    def to_group(src, dst, ssem, rsem, peer):
        return pltpu.make_async_remote_copy(
            src_ref=src, dst_ref=dst, send_sem=ssem, recv_sem=rsem,
            device_id={"expert": peer}, device_id_type=pl.DeviceIdType.MESH,
        )

    def each(n, body):
        def step(i, carry):
            body(i)
            return carry

        lax.fori_loop(0, n, step, 0)

    def span(i, size):
        return pl.ds(pl.multiple_of(i * size, size), size)

    def gate_up_copies(pair):
        slot = lax.rem(pair, depth)
        member, j = lax.div(pair, per_member), lax.rem(pair, per_member)
        where = slice(None) if per_member == 1 else span(j, width)
        return [
            pltpu.make_async_copy(
                ref.at[member, :, where], ring.at[slot, k, 0:features, 0:width], ring_sem.at[slot, k]
            )
            for k, ref in enumerate((gate_ref, up_ref))
        ]

    def down_copies(pair):
        slot = lax.rem(pair, depth)
        c = pair - gu_pairs
        return [
            pltpu.make_async_copy(
                down_ref.at[m, :, span(2 * c + k, DOWN)],
                ring.at[slot, k, m * hidden_units:(m + 1) * hidden_units, 0:DOWN],
                ring_sem.at[slot, k * members + m],
            )
            for k in range(2)
            for m in range(members)
        ]

    def start_pair(pair):
        @pl.when(pair < gu_pairs)
        def _():
            for copy in gate_up_copies(pair):
                copy.start()

        @pl.when(jnp.logical_and(pair >= gu_pairs, pair < total))
        def _():
            for copy in down_copies(pair):
                copy.start()

    barrier = pltpu.get_barrier_semaphore()
    each(shards - 1, lambda d: pl.semaphore_signal(
        barrier, 1, device_id={"shard": shard_peer(d + 1)}, device_id_type=pl.DeviceIdType.MESH))
    each(groups - 1, lambda d: pl.semaphore_signal(
        barrier, 1, device_id={"expert": group_peer(d + 1)}, device_id_type=pl.DeviceIdType.MESH))

    def key_copy(t):
        return pltpu.make_async_copy(key_ref.at[t], keys.at[t], kv_sem.at[0, t])

    def value_copy(t):
        return pltpu.make_async_copy(value_ref.at[t], values.at[t], kv_sem.at[1, t])

    each(count, lambda t: key_copy(t).start())
    each(count, lambda t: value_copy(t).start())
    proj_copy = pltpu.make_async_copy(out_weight_ref, proj, proj_sem)
    proj_copy.start()
    each(depth, start_pair)

    pl.semaphore_wait(barrier, shards - 1 + groups - 1)

    def hid_copy(peer, slot, k):
        return to_shard(
            hidden_ref.at[:, span(peer, cols)], hid_all.at[slot], hid_s.at[k], hid_r.at[slot], peer
        )

    slot_mine = lax.rem(me, quarter)
    sends_hidden = lax.div(me, quarter) == ge

    @pl.when(sends_hidden)
    def _():
        each(shards - 1, lambda d: hid_copy(shard_peer(d + 1), slot_mine, d).start())
        hid_all[slot_mine] = hidden_ref[:, span(me, cols)]

    for t in range(count):
        key_copy(t).wait()
        score[t * heads_local:(t + 1) * heads_local, :] = lax.dot_general(
            queries_ref[t], keys[t], (((1,), (1,)), ((), ())), preferred_element_type=F32
        )
    s = score[...] * (1.0 / math.sqrt(head_size))
    row = lax.broadcasted_iota(jnp.int32, s.shape, 0)
    col = lax.broadcasted_iota(jnp.int32, s.shape, 1)
    mine = lax.rem(col, kv_local) == lax.div(lax.rem(row, heads_local), per_kv)
    s = jnp.where(mine, s, -1e30)
    e = jnp.exp(s - jnp.max(s, axis=1, keepdims=True))
    score[...] = e / jnp.sum(e, axis=1, keepdims=True)
    for t in range(count):
        value_copy(t).wait()
        attended = jnp.dot(
            score[t * heads_local:(t + 1) * heads_local, :].astype(BF16), values[t],
            preferred_element_type=F32,
        )
        for h in range(heads_local):
            heads[t:t + 1, h * head_size:(h + 1) * head_size] = attended[h:h + 1, :]
    att_all[me] = heads[...].astype(BF16)

    def att_copy(slot, peer, k):
        return to_shard(att_all.at[slot], att_all.at[slot], att_s.at[k], att_r.at[slot], peer)

    def send_first(d):
        att_copy(me, shard_peer(d + 1), d).start()

    each(shards - 1, send_first)
    proj_copy.wait()
    each(shards - 1, lambda d: att_copy(shard_peer(d + 1), me, d).wait_recv())

    gathered = att_all[...].astype(F32).reshape(tokens, heads_local * head_size).astype(BF16)
    partial = jnp.dot(gathered, proj[...], preferred_element_type=F32)
    part_send[...] = partial.reshape(shards, count, cols).astype(BF16)

    def part_copy(slot, peer, k):
        return to_group(
            part_send.at[pl.ds(peer * quarter, quarter)], part_recv.at[slot],
            part_s.at[k], part_r.at[slot], peer,
        )

    each(groups - 1, lambda d: part_copy(ge, group_peer(d + 1), d).start())

    def hidden_in(i):
        @pl.when(ge * quarter + i != me)
        def _():
            hid_copy(sibling, i, 0).wait_recv()

    each(quarter, hidden_in)
    summed = hid_all[...].astype(F32) + part_send[pl.ds(ge * quarter, quarter)].astype(F32)
    each(groups - 1, lambda d: part_copy(group_peer(d + 1), group_peer(d + 1), d).wait_recv())
    for d in range(1, groups):
        summed = summed + part_recv[group_peer(d)].astype(F32)
    x_all[pl.ds(ge * quarter, quarter), :, span(me, cols)] = summed.astype(BF16)

    def x_block(g, s):
        return x_all.at[pl.ds(g * quarter, quarter), :, span(s, cols)]

    def x_chip(s, peer, k):
        return to_shard(x_block(ge, s), x_block(ge, s), x_z.at[k], x_r.at[ge, s], peer)

    def x_group(g, s, d, j):
        return to_group(
            x_block(g, s), x_block(g, s), x_g.at[d, j], x_r.at[g, s], group_peer(d + 1)
        )

    def x_core(g, s, d, j):
        return to_shard(x_block(g, s), x_block(g, s), x_c.at[d, j], x_r.at[g, s], sibling)

    def like(j):
        return 2 * chip_peer(j) + core

    def pass_on(j):
        each(groups - 1, lambda d: x_group(ge, like(j), d, j).start())
        x_core(ge, like(j), 0, j).start()

    each(pairs - 1, lambda d: x_chip(me, like(d + 1), d).start())
    pass_on(0)

    def arrived(d):
        x_chip(like(d + 1), sibling, d).wait_recv()
        pass_on(d + 1)

    each(pairs - 1, arrived)

    def across(j):
        def one(d):
            x_group(group_peer(d + 1), like(j), d, j).wait_recv()
            x_core(group_peer(d + 1), like(j), d + 1, j).start()

        each(groups - 1, one)

    each(pairs, across)
    each(pairs, lambda j: each(groups, lambda d: x_core(
        group_peer(d), like(j) + 1 - 2 * core, d, j).wait_recv()))

    square = jnp.zeros((tokens, 1), F32)
    for c in range(chunks):
        x = x_all[:, :, c * chunk:(c + 1) * chunk].astype(F32).reshape(tokens, chunk)
        square = square + jnp.sum(x * x, axis=1, keepdims=True)
    scale = lax.rsqrt(square / features + 1e-05)
    gain = gain_ref[...].astype(F32)
    lanes = gain.shape[1]
    for c in range(gain.shape[0]):
        part = slice(c * lanes, (c + 1) * lanes)
        x = x_all[:, :, part].astype(F32).reshape(tokens, lanes)
        normed[:, part] = (x * scale * gain[c:c + 1]).astype(BF16)

    logits = lax.dot_general(
        normed[...], router_ref[...], (((1,), (1,)), ((), ())), preferred_element_type=F32
    )
    diagonal = lax.broadcasted_iota(jnp.int32, (tokens, tokens), 0) == lax.broadcasted_iota(
        jnp.int32, (tokens, tokens), 1
    )
    first, second = (
        jnp.sum(
            jnp.where(diagonal, ids_ref[k:k + 1, :].astype(F32), 0.0), axis=1, keepdims=True
        ).astype(jnp.int32)
        for k in range(2)
    )
    lane = lax.broadcasted_iota(jnp.int32, logits.shape, 1)
    top_first = jnp.sum(jnp.where(lane == first, logits, 0.0), axis=1, keepdims=True)
    top_second = jnp.sum(jnp.where(lane == second, logits, 0.0), axis=1, keepdims=True)
    weight_first = 1.0 / (1.0 + jnp.exp(top_second - top_first))
    weight_second = 1.0 / (1.0 + jnp.exp(top_first - top_second))
    for m in range(members):
        expert = ge * members + m
        route[m] = jnp.broadcast_to(
            jnp.where(first == expert, weight_first, 0.0)
            + jnp.where(second == expert, weight_second, 0.0),
            (tokens, 128),
        )

    def gate_up(pair):
        slot = lax.rem(pair, depth)
        member, j = lax.div(pair, per_member), lax.rem(pair, per_member)
        for copy in gate_up_copies(pair):
            copy.wait()
        gated = jnp.dot(
            normed[...], ring[slot, 0, 0:features, 0:width], preferred_element_type=F32
        )
        upward = jnp.dot(
            normed[...], ring[slot, 1, 0:features, 0:width], preferred_element_type=F32
        )
        value = gated * (1.0 / (1.0 + jnp.exp(-gated))) * upward * route[member][:, 0:1]
        where = slice(None) if per_member == 1 else span(j, width)
        act[member, :, where] = value.astype(BF16)
        start_pair(pair + depth)

    each(gu_pairs, gate_up)

    half = DOWN

    def core_copy(c):
        return to_shard(
            part_out.at[:, :, span(2 * c + 1 - core, half)], core_in.at[:, :, span(c, half)],
            i_s.at[c], i_r.at[c], sibling,
        )

    def chip_copy(c, slot, dest, k):
        return to_shard(
            core_sum.at[pl.ds(2 * dest, 2), :, span(c, half)], chip_in.at[slot, :, :, span(c, half)],
            a_s.at[k, c], a_r.at[slot, c], 2 * dest + core,
        )

    def b_copy(c, slot, peer, k):
        ref = group.at[slot, :, :, span(c, half)]
        return to_group(ref, ref, b_s.at[k, c], b_r.at[slot, c], peer)

    def final_copy(c, block):
        ref = final.at[block, :, span(2 * c + 1 - block, half)]
        return to_shard(ref, ref, f_s.at[c], f_r.at[c], sibling)

    def sum_cores(c):
        core_copy(c).wait_recv()
        core_sum[:, :, span(c, half)] = (
            part_out[:, :, span(2 * c + core, half)].astype(F32)
            + core_in[:, :, span(c, half)].astype(F32)
        ).astype(BF16)
        each(pairs - 1, lambda d: chip_copy(c, chip, chip_peer(d + 1), d).start())

    def sum_chips(c):
        each(pairs - 1, lambda d: chip_copy(c, chip_peer(d + 1), chip_peer(d + 1), d).wait_recv())
        mix = core_sum[pl.ds(2 * chip, 2), :, span(c, half)].astype(F32)
        for d in range(1, pairs):
            mix = mix + chip_in[chip_peer(d), :, :, span(c, half)].astype(F32)
        group[ge, :, :, span(c, half)] = mix.astype(BF16)
        each(groups - 1, lambda d: b_copy(c, ge, group_peer(d + 1), d).start())

    def sum_groups(c):
        each(groups - 1, lambda d: b_copy(c, group_peer(d + 1), group_peer(d + 1), d).wait_recv())
        mix = group[0, :, :, span(c, half)].astype(F32)
        for g in range(1, groups):
            mix = mix + group[g, :, :, span(c, half)].astype(F32)
        where = span(2 * c + core, half)
        mix = mix + x_all[pl.ds(2 * chip, 2), :, where].astype(F32)
        final[:, :, where] = mix.astype(BF16)
        final_copy(c, 1 - core).start()

    def down(c):
        pair = gu_pairs + c
        slot = lax.rem(pair, depth)
        for copy in down_copies(pair):
            copy.wait()
        for k in range(2):
            y = jnp.zeros((tokens, DOWN), F32)
            for m in range(members):
                y = y + jnp.dot(
                    act[m],
                    ring[slot, k, m * hidden_units:(m + 1) * hidden_units, 0:DOWN],
                    preferred_element_type=F32,
                )
            part_out[:, :, span(2 * c + k, DOWN)] = y.reshape(shards, count, DOWN).astype(BF16)
        core_copy(c).start()
        start_pair(pair + depth)

    def stage(t):
        @pl.when(t < chunks)
        def _():
            down(t)

        for lag, work in ((1, sum_cores), (2, sum_chips), (3, sum_groups)):
            @pl.when(jnp.logical_and(t >= lag, t < chunks + lag))
            def _():
                work(t - lag)

    each(chunks + 3, stage)
    each(chunks, lambda c: final_copy(c, core).wait_recv())
    out_ref[...] = final[core]

    each(shards - 1, lambda d: att_copy(me, shard_peer(d + 1), d).wait_send())

    @pl.when(sends_hidden)
    def _():
        each(shards - 1, lambda d: hid_copy(shard_peer(d + 1), slot_mine, d).wait_send())

    each(groups - 1, lambda d: part_copy(ge, group_peer(d + 1), d).wait_send())
    each(pairs - 1, lambda d: x_chip(me, like(d + 1), d).wait_send())
    each(pairs, lambda j: each(groups - 1, lambda d: x_group(ge, like(j), d, j).wait_send()))
    each(pairs, lambda j: each(groups, lambda d: x_core(
        group_peer(d), like(j), d, j).wait_send()))

    def sent(c):
        core_copy(c).wait_send()
        final_copy(c, 1 - core).wait_send()
        each(pairs - 1, lambda d: chip_copy(c, chip, chip_peer(d + 1), d).wait_send())
        each(groups - 1, lambda d: b_copy(c, ge, group_peer(d + 1), d).wait_send())

    each(chunks, sent)


def on_device(
    shards,
    groups,
    hidden,
    queries,
    key_cache,
    value_cache,
    out_weight,
    norm_gain,
    router,
    expert_ids,
    gate_weight,
    up_weight,
    down_weight,
):
    count, features = hidden.shape
    _, heads_local, head_size = queries.shape
    _, positions, kv_local, _ = key_cache.shape
    members, _, hidden_units = gate_weight.shape
    tokens = count * shards
    cols = features // shards
    rows = positions * kv_local
    width = 256 if hidden_units % 256 == 0 else hidden_units
    lanes = max(width, DOWN)
    deep = max(features, members * hidden_units)
    chunks = features // (2 * DOWN)
    total = members * (hidden_units // width) + chunks
    pair_bytes = 2 * 2 * deep * (-(-lanes // 128) * 128)
    fixed = 2 * (
        2 * count * rows * head_size + out_weight.size + 4 * tokens * features
        + (groups + 2) * tokens * cols + members * tokens * hidden_units
        + (2 * count + groups * count) * features + 2 * count * heads_local * rows
    )
    depth = min(total, (VMEM_BYTES - fixed) // pair_bytes)
    sizes = (shards, groups, depth, width, kv_local)
    vmem = pl.BlockSpec(memory_space=pltpu.VMEM)
    hbm = pl.BlockSpec(memory_space=pl.ANY)
    sem = pltpu.SemaphoreType.DMA
    return pl.pallas_call(
        functools.partial(layer_kernel, sizes),
        out_shape=jax.ShapeDtypeStruct((count, features), BF16),
        in_specs=[vmem, vmem, hbm, hbm, hbm, vmem, vmem, vmem, hbm, hbm, hbm],
        out_specs=vmem,
        scratch_shapes=[
            pltpu.VMEM((depth, 2, deep, lanes), BF16),
            pltpu.VMEM((count, rows, head_size), BF16),
            pltpu.VMEM((count, rows, head_size), BF16),
            pltpu.VMEM(out_weight.shape, BF16),
            pltpu.VMEM((count * heads_local, rows), F32),
            pltpu.VMEM((count, heads_local * head_size), F32),
            pltpu.VMEM((shards, count, heads_local * head_size), BF16),
            pltpu.VMEM((shards // groups, count, cols), BF16),
            pltpu.VMEM((shards, count, cols), BF16),
            pltpu.VMEM((groups, shards // groups, count, cols), BF16),
            pltpu.VMEM((shards, count, features), BF16),
            pltpu.VMEM((tokens, features), BF16),
            pltpu.VMEM((members, tokens, 128), F32),
            pltpu.VMEM((members, tokens, hidden_units), BF16),
            pltpu.VMEM((shards, count, features), BF16),
            pltpu.VMEM((shards, count, features // 2), BF16),
            pltpu.VMEM((shards, count, features // 2), BF16),
            pltpu.VMEM((shards // 2, 2, count, features // 2), BF16),
            pltpu.VMEM((groups, 2, count, features // 2), BF16),
            pltpu.VMEM((2, count, features), BF16),
            sem((depth, 2 * members)),
            sem((2, count)),
            sem,
            sem((shards,)),
            sem((shards,)),
            sem((shards,)),
            sem((shards // groups,)),
            sem((groups,)),
            sem((groups,)),
            sem((shards // 2,)),
            sem((groups, shards // 2)),
            sem((groups, shards // 2)),
            sem((groups, shards)),
            sem((chunks,)),
            sem((chunks,)),
            sem((shards // 2, chunks)),
            sem((shards // 2, chunks)),
            sem((groups, chunks)),
            sem((groups, chunks)),
            sem((chunks,)),
            sem((chunks,)),
        ],
        compiler_params=pltpu.CompilerParams(
            collective_id=0, has_side_effects=True, vmem_limit_bytes=67043328
        ),
        name="layer",
    )(
        hidden,
        queries,
        key_cache.reshape(count, rows, head_size),
        value_cache.reshape(count, rows, head_size),
        out_weight,
        norm_gain.reshape(features // 128, 128),
        router.T,
        expert_ids.T,
        gate_weight,
        up_weight,
        down_weight,
    )


def solution(mesh):
    in_specs = (
        P("shard", None),
        P("shard", "expert", None),
        P("shard", None, "expert", None),
        P("shard", None, "expert", None),
        P("expert", "shard"),
        P(),
        P(),
        P(),
        P("expert", None, "shard"),
        P("expert", None, "shard"),
        P("expert", "shard", None),
    )
    body = functools.partial(on_device, mesh.shape["shard"], mesh.shape["expert"])
    return jax.shard_map(
        body, mesh=mesh, in_specs=in_specs, out_specs=P("shard", None), check_vma=False
    )
```

```python
import functools
import math

import jax
import jax.numpy as jnp
from jax import lax
from jax.experimental import pallas as pl
from jax.experimental.pallas import tpu as pltpu
from jax.sharding import PartitionSpec as P

F32 = jnp.float32
BF16 = jnp.bfloat16
VMEM_BYTES = 61 * 1024 * 1024
DOWN = 256


def layer_kernel(
    sizes,
    hidden_ref,
    queries_ref,
    key_ref,
    value_ref,
    out_weight_ref,
    gain_ref,
    router_ref,
    ids_ref,
    gate_ref,
    up_ref,
    down_ref,
    out_ref,
    ring,
    keys,
    values,
    proj,
    score,
    heads,
    att_all,
    hid_all,
    part_send,
    part_recv,
    x_all,
    normed,
    route,
    act,
    part_out,
    core_in,
    core_sum,
    chip_in,
    group,
    final,
    ring_sem,
    kv_sem,
    proj_sem,
    att_s,
    att_r,
    hid_s,
    hid_r,
    part_s,
    part_r,
    x_z,
    x_g,
    x_c,
    x_r,
    i_s,
    i_r,
    a_s,
    a_r,
    b_s,
    b_r,
    f_s,
    f_r,
):
    shards, groups, depth, width, kv_local = sizes
    me = lax.axis_index("shard")
    ge = lax.axis_index("expert")
    count, features = hidden_ref.shape
    tokens = count * shards
    cols = features // shards
    members, _, hidden_units = gate_ref.shape
    per_member = hidden_units // width
    gu_pairs = members * per_member
    chunk = 2 * DOWN
    chunks = features // chunk
    total = gu_pairs + chunks
    heads_local, head_size = queries_ref.shape[1:]
    per_kv = heads_local // kv_local
    quarter = shards // groups
    pairs = shards // 2
    core = lax.rem(me, 2)
    chip = lax.div(me, 2)
    sibling = me + 1 - 2 * core

    def shard_peer(d):
        return lax.rem(me + d, shards)

    def group_peer(d):
        return lax.rem(ge + d, groups)

    def chip_peer(d):
        return lax.rem(chip + d, pairs)

    def to_shard(src, dst, ssem, rsem, peer):
        return pltpu.make_async_remote_copy(
            src_ref=src, dst_ref=dst, send_sem=ssem, recv_sem=rsem,
            device_id={"shard": peer}, device_id_type=pl.DeviceIdType.MESH,
        )

    def to_group(src, dst, ssem, rsem, peer):
        return pltpu.make_async_remote_copy(
            src_ref=src, dst_ref=dst, send_sem=ssem, recv_sem=rsem,
            device_id={"expert": peer}, device_id_type=pl.DeviceIdType.MESH,
        )

    def each(n, body):
        def step(i, carry):
            body(i)
            return carry

        lax.fori_loop(0, n, step, 0)

    def span(i, size):
        return pl.ds(pl.multiple_of(i * size, size), size)

    def gate_up_copies(pair):
        slot = lax.rem(pair, depth)
        member, j = lax.div(pair, per_member), lax.rem(pair, per_member)
        where = slice(None) if per_member == 1 else span(j, width)
        return [
            pltpu.make_async_copy(
                ref.at[member, :, where], ring.at[slot, k, 0:features, 0:width], ring_sem.at[slot, k]
            )
            for k, ref in enumerate((gate_ref, up_ref))
        ]

    def down_copies(pair):
        slot = lax.rem(pair, depth)
        c = pair - gu_pairs
        return [
            pltpu.make_async_copy(
                down_ref.at[m, :, span(2 * c + k, DOWN)],
                ring.at[slot, k, m * hidden_units:(m + 1) * hidden_units, 0:DOWN],
                ring_sem.at[slot, k * members + m],
            )
            for k in range(2)
            for m in range(members)
        ]

    def start_pair(pair):
        @pl.when(pair < gu_pairs)
        def _():
            for copy in gate_up_copies(pair):
                copy.start()

        @pl.when(jnp.logical_and(pair >= gu_pairs, pair < total))
        def _():
            for copy in down_copies(pair):
                copy.start()

    barrier = pltpu.get_barrier_semaphore()
    each(shards - 1, lambda d: pl.semaphore_signal(
        barrier, 1, device_id={"shard": shard_peer(d + 1)}, device_id_type=pl.DeviceIdType.MESH))
    each(groups - 1, lambda d: pl.semaphore_signal(
        barrier, 1, device_id={"expert": group_peer(d + 1)}, device_id_type=pl.DeviceIdType.MESH))

    def key_copy(t):
        return pltpu.make_async_copy(key_ref.at[t], keys.at[t], kv_sem.at[0, t])

    def value_copy(t):
        return pltpu.make_async_copy(value_ref.at[t], values.at[t], kv_sem.at[1, t])

    each(count, lambda t: key_copy(t).start())
    each(count, lambda t: value_copy(t).start())
    proj_copy = pltpu.make_async_copy(out_weight_ref, proj, proj_sem)
    proj_copy.start()
    each(depth, start_pair)

    pl.semaphore_wait(barrier, shards - 1 + groups - 1)

    def hid_copy(peer, slot, k):
        return to_shard(
            hidden_ref.at[:, span(peer, cols)], hid_all.at[slot], hid_s.at[k], hid_r.at[slot], peer
        )

    slot_mine = lax.rem(me, quarter)
    sends_hidden = lax.div(me, quarter) == ge

    @pl.when(sends_hidden)
    def _():
        each(shards - 1, lambda d: hid_copy(shard_peer(d + 1), slot_mine, d).start())
        hid_all[slot_mine] = hidden_ref[:, span(me, cols)]

    for t in range(count):
        key_copy(t).wait()
        score[t * heads_local:(t + 1) * heads_local, :] = lax.dot_general(
            queries_ref[t], keys[t], (((1,), (1,)), ((), ())), preferred_element_type=F32
        )
    s = score[...] * (1.0 / math.sqrt(head_size))
    row = lax.broadcasted_iota(jnp.int32, s.shape, 0)
    col = lax.broadcasted_iota(jnp.int32, s.shape, 1)
    mine = lax.rem(col, kv_local) == lax.div(lax.rem(row, heads_local), per_kv)
    s = jnp.where(mine, s, -1e30)
    e = jnp.exp(s - jnp.max(s, axis=1, keepdims=True))
    score[...] = e / jnp.sum(e, axis=1, keepdims=True)
    for t in range(count):
        value_copy(t).wait()
        attended = jnp.dot(
            score[t * heads_local:(t + 1) * heads_local, :].astype(BF16), values[t],
            preferred_element_type=F32,
        )
        for h in range(heads_local):
            heads[t:t + 1, h * head_size:(h + 1) * head_size] = attended[h:h + 1, :]
    att_all[me] = heads[...].astype(BF16)

    def att_copy(slot, peer, k):
        return to_shard(att_all.at[slot], att_all.at[slot], att_s.at[k], att_r.at[slot], peer)

    def send_first(d):
        att_copy(me, shard_peer(d + 1), d).start()

    each(shards - 1, send_first)
    proj_copy.wait()
    each(shards - 1, lambda d: att_copy(shard_peer(d + 1), me, d).wait_recv())

    gathered = att_all[...].astype(F32).reshape(tokens, heads_local * head_size).astype(BF16)
    partial = jnp.dot(gathered, proj[...], preferred_element_type=F32)
    part_send[...] = partial.reshape(shards, count, cols).astype(BF16)

    def part_copy(slot, peer, k):
        return to_group(
            part_send.at[pl.ds(peer * quarter, quarter)], part_recv.at[slot],
            part_s.at[k], part_r.at[slot], peer,
        )

    each(groups - 1, lambda d: part_copy(ge, group_peer(d + 1), d).start())

    def hidden_in(i):
        @pl.when(ge * quarter + i != me)
        def _():
            hid_copy(sibling, i, 0).wait_recv()

    each(quarter, hidden_in)
    summed = hid_all[...].astype(F32) + part_send[pl.ds(ge * quarter, quarter)].astype(F32)
    each(groups - 1, lambda d: part_copy(group_peer(d + 1), group_peer(d + 1), d).wait_recv())
    for d in range(1, groups):
        summed = summed + part_recv[group_peer(d)].astype(F32)
    x_all[pl.ds(ge * quarter, quarter), :, span(me, cols)] = summed.astype(BF16)

    def x_block(g, s):
        return x_all.at[pl.ds(g * quarter, quarter), :, span(s, cols)]

    def x_chip(s, peer, k):
        return to_shard(x_block(ge, s), x_block(ge, s), x_z.at[k], x_r.at[ge, s], peer)

    def x_group(g, s, d, j):
        return to_group(
            x_block(g, s), x_block(g, s), x_g.at[d, j], x_r.at[g, s], group_peer(d + 1)
        )

    def x_core(g, s, d, j):
        return to_shard(x_block(g, s), x_block(g, s), x_c.at[d, j], x_r.at[g, s], sibling)

    def like(j):
        return 2 * chip_peer(j) + core

    def pass_on(j):
        each(groups - 1, lambda d: x_group(ge, like(j), d, j).start())
        x_core(ge, like(j), 0, j).start()

    each(pairs - 1, lambda d: x_chip(me, like(d + 1), d).start())
    pass_on(0)

    def arrived(d):
        x_chip(like(d + 1), sibling, d).wait_recv()
        pass_on(d + 1)

    each(pairs - 1, arrived)

    def across(j):
        def one(d):
            x_group(group_peer(d + 1), like(j), d, j).wait_recv()
            x_core(group_peer(d + 1), like(j), d + 1, j).start()

        each(groups - 1, one)

    each(pairs, across)
    each(pairs, lambda j: each(groups, lambda d: x_core(
        group_peer(d), like(j) + 1 - 2 * core, d, j).wait_recv()))

    square = jnp.zeros((tokens, 1), F32)
    for c in range(chunks):
        x = x_all[:, :, c * chunk:(c + 1) * chunk].astype(F32).reshape(tokens, chunk)
        square = square + jnp.sum(x * x, axis=1, keepdims=True)
    scale = lax.rsqrt(square / features + 1e-05)
    gain = gain_ref[...].astype(F32)
    lanes = gain.shape[1]
    for c in range(gain.shape[0]):
        part = slice(c * lanes, (c + 1) * lanes)
        x = x_all[:, :, part].astype(F32).reshape(tokens, lanes)
        normed[:, part] = (x * scale * gain[c:c + 1]).astype(BF16)

    logits = lax.dot_general(
        normed[...], router_ref[...], (((1,), (1,)), ((), ())), preferred_element_type=F32
    )
    diagonal = lax.broadcasted_iota(jnp.int32, (tokens, tokens), 0) == lax.broadcasted_iota(
        jnp.int32, (tokens, tokens), 1
    )
    first, second = (
        jnp.sum(
            jnp.where(diagonal, ids_ref[k:k + 1, :].astype(F32), 0.0), axis=1, keepdims=True
        ).astype(jnp.int32)
        for k in range(2)
    )
    lane = lax.broadcasted_iota(jnp.int32, logits.shape, 1)
    top_first = jnp.sum(jnp.where(lane == first, logits, 0.0), axis=1, keepdims=True)
    top_second = jnp.sum(jnp.where(lane == second, logits, 0.0), axis=1, keepdims=True)
    weight_first = 1.0 / (1.0 + jnp.exp(top_second - top_first))
    weight_second = 1.0 / (1.0 + jnp.exp(top_first - top_second))
    for m in range(members):
        expert = ge * members + m
        route[m] = jnp.broadcast_to(
            jnp.where(first == expert, weight_first, 0.0)
            + jnp.where(second == expert, weight_second, 0.0),
            (tokens, 128),
        )

    def gate_up(pair):
        slot = lax.rem(pair, depth)
        member, j = lax.div(pair, per_member), lax.rem(pair, per_member)
        for copy in gate_up_copies(pair):
            copy.wait()
        gated = jnp.dot(
            normed[...], ring[slot, 0, 0:features, 0:width], preferred_element_type=F32
        )
        upward = jnp.dot(
            normed[...], ring[slot, 1, 0:features, 0:width], preferred_element_type=F32
        )
        value = gated * (1.0 / (1.0 + jnp.exp(-gated))) * upward * route[member][:, 0:1]
        where = slice(None) if per_member == 1 else span(j, width)
        act[member, :, where] = value.astype(BF16)
        start_pair(pair + depth)

    each(gu_pairs, gate_up)

    half = DOWN

    def core_copy(c):
        return to_shard(
            part_out.at[:, :, span(2 * c + 1 - core, half)], core_in.at[:, :, span(c, half)],
            i_s.at[c], i_r.at[c], sibling,
        )

    def chip_copy(c, slot, dest, k):
        return to_shard(
            core_sum.at[pl.ds(2 * dest, 2), :, span(c, half)], chip_in.at[slot, :, :, span(c, half)],
            a_s.at[k, c], a_r.at[slot, c], 2 * dest + core,
        )

    def b_copy(c, slot, peer, k):
        ref = group.at[slot, :, :, span(c, half)]
        return to_group(ref, ref, b_s.at[k, c], b_r.at[slot, c], peer)

    def final_copy(c, block):
        ref = final.at[block, :, span(2 * c + 1 - block, half)]
        return to_shard(ref, ref, f_s.at[c], f_r.at[c], sibling)

    def sum_cores(c):
        core_copy(c).wait_recv()
        core_sum[:, :, span(c, half)] = (
            part_out[:, :, span(2 * c + core, half)].astype(F32)
            + core_in[:, :, span(c, half)].astype(F32)
        ).astype(BF16)
        each(pairs - 1, lambda d: chip_copy(c, chip, chip_peer(d + 1), d).start())

    def sum_chips(c):
        each(pairs - 1, lambda d: chip_copy(c, chip_peer(d + 1), chip_peer(d + 1), d).wait_recv())
        mix = core_sum[pl.ds(2 * chip, 2), :, span(c, half)].astype(F32)
        for d in range(1, pairs):
            mix = mix + chip_in[chip_peer(d), :, :, span(c, half)].astype(F32)
        group[ge, :, :, span(c, half)] = mix.astype(BF16)
        each(groups - 1, lambda d: b_copy(c, ge, group_peer(d + 1), d).start())

    def sum_groups(c):
        each(groups - 1, lambda d: b_copy(c, group_peer(d + 1), group_peer(d + 1), d).wait_recv())
        mix = group[0, :, :, span(c, half)].astype(F32)
        for g in range(1, groups):
            mix = mix + group[g, :, :, span(c, half)].astype(F32)
        where = span(2 * c + core, half)
        mix = mix + x_all[pl.ds(2 * chip, 2), :, where].astype(F32)
        final[:, :, where] = mix.astype(BF16)
        final_copy(c, 1 - core).start()

    def down(c):
        pair = gu_pairs + c
        slot = lax.rem(pair, depth)
        for copy in down_copies(pair):
            copy.wait()
        for k in range(2):
            y = jnp.zeros((tokens, DOWN), F32)
            for m in range(members):
                y = y + jnp.dot(
                    act[m],
                    ring[slot, k, m * hidden_units:(m + 1) * hidden_units, 0:DOWN],
                    preferred_element_type=F32,
                )
            part_out[:, :, span(2 * c + k, DOWN)] = y.reshape(shards, count, DOWN).astype(BF16)
        core_copy(c).start()
        start_pair(pair + depth)

    def stage(t):
        @pl.when(t < chunks)
        def _():
            down(t)

        for lag, work in ((1, sum_cores), (4, sum_chips), (6, sum_groups)):
            @pl.when(jnp.logical_and(t >= lag, t < chunks + lag))
            def _():
                work(t - lag)

    each(chunks + 6, stage)
    each(chunks, lambda c: final_copy(c, core).wait_recv())
    out_ref[...] = final[core]

    each(shards - 1, lambda d: att_copy(me, shard_peer(d + 1), d).wait_send())

    @pl.when(sends_hidden)
    def _():
        each(shards - 1, lambda d: hid_copy(shard_peer(d + 1), slot_mine, d).wait_send())

    each(groups - 1, lambda d: part_copy(ge, group_peer(d + 1), d).wait_send())
    each(pairs - 1, lambda d: x_chip(me, like(d + 1), d).wait_send())
    each(pairs, lambda j: each(groups - 1, lambda d: x_group(ge, like(j), d, j).wait_send()))
    each(pairs, lambda j: each(groups, lambda d: x_core(
        group_peer(d), like(j), d, j).wait_send()))

    def sent(c):
        core_copy(c).wait_send()
        final_copy(c, 1 - core).wait_send()
        each(pairs - 1, lambda d: chip_copy(c, chip, chip_peer(d + 1), d).wait_send())
        each(groups - 1, lambda d: b_copy(c, ge, group_peer(d + 1), d).wait_send())

    each(chunks, sent)


def on_device(
    shards,
    groups,
    hidden,
    queries,
    key_cache,
    value_cache,
    out_weight,
    norm_gain,
    router,
    expert_ids,
    gate_weight,
    up_weight,
    down_weight,
):
    count, features = hidden.shape
    _, heads_local, head_size = queries.shape
    _, positions, kv_local, _ = key_cache.shape
    members, _, hidden_units = gate_weight.shape
    tokens = count * shards
    cols = features // shards
    rows = positions * kv_local
    width = 256 if hidden_units % 256 == 0 else hidden_units
    lanes = max(width, DOWN)
    deep = max(features, members * hidden_units)
    chunks = features // (2 * DOWN)
    total = members * (hidden_units // width) + chunks
    pair_bytes = 2 * 2 * deep * (-(-lanes // 128) * 128)
    fixed = 2 * (
        2 * count * rows * head_size + out_weight.size + 4 * tokens * features
        + (groups + 2) * tokens * cols + members * tokens * hidden_units
        + (2 * count + groups * count) * features + 2 * count * heads_local * rows
    )
    depth = min(total, (VMEM_BYTES - fixed) // pair_bytes)
    sizes = (shards, groups, depth, width, kv_local)
    vmem = pl.BlockSpec(memory_space=pltpu.VMEM)
    hbm = pl.BlockSpec(memory_space=pl.ANY)
    sem = pltpu.SemaphoreType.DMA
    return pl.pallas_call(
        functools.partial(layer_kernel, sizes),
        out_shape=jax.ShapeDtypeStruct((count, features), BF16),
        in_specs=[vmem, vmem, hbm, hbm, hbm, vmem, vmem, vmem, hbm, hbm, hbm],
        out_specs=vmem,
        scratch_shapes=[
            pltpu.VMEM((depth, 2, deep, lanes), BF16),
            pltpu.VMEM((count, rows, head_size), BF16),
            pltpu.VMEM((count, rows, head_size), BF16),
            pltpu.VMEM(out_weight.shape, BF16),
            pltpu.VMEM((count * heads_local, rows), F32),
            pltpu.VMEM((count, heads_local * head_size), F32),
            pltpu.VMEM((shards, count, heads_local * head_size), BF16),
            pltpu.VMEM((shards // groups, count, cols), BF16),
            pltpu.VMEM((shards, count, cols), BF16),
            pltpu.VMEM((groups, shards // groups, count, cols), BF16),
            pltpu.VMEM((shards, count, features), BF16),
            pltpu.VMEM((tokens, features), BF16),
            pltpu.VMEM((members, tokens, 128), F32),
            pltpu.VMEM((members, tokens, hidden_units), BF16),
            pltpu.VMEM((shards, count, features), BF16),
            pltpu.VMEM((shards, count, features // 2), BF16),
            pltpu.VMEM((shards, count, features // 2), BF16),
            pltpu.VMEM((shards // 2, 2, count, features // 2), BF16),
            pltpu.VMEM((groups, 2, count, features // 2), BF16),
            pltpu.VMEM((2, count, features), BF16),
            sem((depth, 2 * members)),
            sem((2, count)),
            sem,
            sem((shards,)),
            sem((shards,)),
            sem((shards,)),
            sem((shards // groups,)),
            sem((groups,)),
            sem((groups,)),
            sem((shards // 2,)),
            sem((groups, shards // 2)),
            sem((groups, shards // 2)),
            sem((groups, shards)),
            sem((chunks,)),
            sem((chunks,)),
            sem((shards // 2, chunks)),
            sem((shards // 2, chunks)),
            sem((groups, chunks)),
            sem((groups, chunks)),
            sem((chunks,)),
            sem((chunks,)),
        ],
        compiler_params=pltpu.CompilerParams(
            collective_id=0, has_side_effects=True, vmem_limit_bytes=67043328
        ),
        name="layer",
    )(
        hidden,
        queries,
        key_cache.reshape(count, rows, head_size),
        value_cache.reshape(count, rows, head_size),
        out_weight,
        norm_gain.reshape(features // 128, 128),
        router.T,
        expert_ids.T,
        gate_weight,
        up_weight,
        down_weight,
    )


def solution(mesh):
    in_specs = (
        P("shard", None),
        P("shard", "expert", None),
        P("shard", None, "expert", None),
        P("shard", None, "expert", None),
        P("expert", "shard"),
        P(),
        P(),
        P(),
        P("expert", None, "shard"),
        P("expert", None, "shard"),
        P("expert", "shard", None),
    )
    body = functools.partial(on_device, mesh.shape["shard"], mesh.shape["expert"])
    return jax.shard_map(
        body, mesh=mesh, in_specs=in_specs, out_specs=P("shard", None), check_vma=False
    )
```
